32 devices in a mesh: dom: 16 (over z, y, x), band: 2 (over core).
Axes of the slice: x: 2, y: 2, z: 4, core: 2. Of those that a mesh axis runs over, the one named last changes fastest.
Arguments:
- wavefunctions: bfloat16 [32768, 1024], P('dom', 'band'), may hold values from -4 to 4
- mass_scale: float32 [32768], P('dom'), may hold values from 0.7 to 1.4
- cell_matrices: bfloat16 [128, 512, 512], P('dom')
- connectivity: int32 [128, 512], P('dom'), may hold values from 0 to 2303, as said below
- face_index: int32 [4096], P('dom'), may hold values from 0 to 2047, as said below
Outputs:
- rotated: float32 [32768, 1024], P('dom', 'band')
The draws below stay inside these ranges and needn't reach their ends.
Inputs may be any that keep to these rules, and one draw needn't show every extreme that they name: `connectivity`: local numbers of each cell's 512 nodes within its domain: below 2048 the domain's own nodes, from 2048 on the entries of the next domain's face list in order; every local number appears in its domain, and a number may repeat. `face_index`: local numbers of 256 own nodes of each domain, in the order that the previous domain uses; a number may repeat.
All inputs are finite; a program needn't handle non-finite values.
Results may differ from the reference program's by a relative error of at most 0.011.
Values may be sent and summed in bfloat16 or wider, within the bound.
A program may use at most 64 MiB of HBM per device.

```python
import math
import jax
import jax.numpy as jnp
from jax import lax

NODE_DEV = 2048
STATES = 1024
CELL_NODES = 512
DEGREE = 3
NS_ITERS = 2
CELLS_DEV = 8
FACE = 256
NODES = 32768
CELLS = 128
FACES = 4096
N_DOM = 16


def draw_wavefunctions(key, part):
    key_one = jax.random.fold_in(jax.random.fold_in(key, 5), 0)
    values = jax.random.truncated_normal(key_one, -4.0, 4.0, (NODES, STATES), jnp.float32)
    return jnp.clip(values, -4.0, 4.0).astype(jnp.bfloat16)


def draw_cell_matrices(key, part):
    key_one, key_two = jax.random.split(jax.random.fold_in(key, 3))
    cell_shape = (CELLS, CELL_NODES, CELL_NODES)
    random_part = jax.random.normal(key_one, cell_shape, jnp.float32)
    diagonal = jax.random.uniform(key_two, (CELLS, CELL_NODES), jnp.float32, 0.5, 2.5)
    symmetric = (random_part + jnp.swapaxes(random_part, 1, 2)) / (2.0 * math.sqrt(CELL_NODES))
    identity = jnp.eye(CELL_NODES, dtype=jnp.float32)
    return (symmetric + diagonal[:, :, None] * identity[None]).astype(jnp.bfloat16)


def draw_connectivity(key, part):
    domains = CELLS // CELLS_DEV
    extent = NODE_DEV + FACE

    def one_domain(domain_key):
        key_one, key_two = jax.random.split(domain_key)
        ordering = jnp.concatenate([jax.random.permutation(key_one, extent), jax.random.permutation(key_two, extent)])
        return ordering[:CELLS_DEV * CELL_NODES].reshape(CELLS_DEV, CELL_NODES)
    domain_keys = jax.random.split(jax.random.fold_in(key, 11), domains)
    return jax.vmap(one_domain)(domain_keys).reshape(CELLS, CELL_NODES).astype(jnp.int32)


def draw_face_index(key, part):
    domains = FACES // FACE

    def one_domain(domain_key):
        chosen = jax.random.permutation(domain_key, NODE_DEV)[:FACE]
        return chosen.at[0].set(NODE_DEV - 1)
    domain_keys = jax.random.split(jax.random.fold_in(key, 17), domains)
    return jax.vmap(one_domain)(domain_keys).reshape(FACES).astype(jnp.int32)


def steps_of(rng, shape, shards, least, high):
    level = 1.0
    for dim, shards_of in shards:
        draws = jax.random.uniform(jax.random.fold_in(jax.random.fold_in(rng, 6), dim), (shards_of,), jnp.float32, least / len(shards), high / len(shards))
        level = level * jnp.repeat(jnp.exp(draws), shape[dim] // shards_of).reshape((-1,) + (1,) * (len(shape) - 1 - dim))
    return level


def setup_inputs(seed: int = 0) -> dict:
    splits = jax.random.split(jax.random.key(seed), 6)
    return {
        "wavefunctions": draw_wavefunctions(jax.random.fold_in(splits[5], 71), 0),
        "mass_scale": jnp.clip(jnp.exp(math.log(1.4) - 0.6931472 * jax.random.uniform(splits[1], (NODES,), jnp.float32) ** steps_of(splits[1], (NODES,), ((0, 16),), -0.2, 0.2)), 0.7, 1.4),
        "cell_matrices": draw_cell_matrices(jax.random.fold_in(splits[5], 71), 0),
        "connectivity": draw_connectivity(jax.random.fold_in(splits[5], 71), 0),
        "face_index": draw_face_index(jax.random.fold_in(splits[5], 71), 0),
    }


def apply_hamiltonian(vectors, mass_scale, cell_matrices, connectivity, face_index):
    band_width = vectors.shape[1]
    scaled = (mass_scale[:, None] * vectors).astype(jnp.bfloat16)
    by_domain = scaled.reshape(N_DOM, NODE_DEV, band_width)
    face_lists = face_index.reshape(N_DOM, FACE)
    face_rows = jax.vmap(lambda rows_all, picks: jnp.take(rows_all, picks, axis=0))(by_domain, face_lists)
    received = jnp.concatenate([face_rows[1:], jnp.zeros_like(face_rows[:1])], axis=0)
    extended = jnp.concatenate([by_domain, received], axis=1)
    cell_blocks = cell_matrices.reshape(N_DOM, CELLS_DEV, CELL_NODES, CELL_NODES)
    link_blocks = connectivity.reshape(N_DOM, CELLS_DEV, CELL_NODES)

    def one_domain(inputs):
        extended_rows, matrices, links = inputs
        gathered = jnp.take(extended_rows, links, axis=0).astype(jnp.float32)
        products = jnp.einsum('cij,cjs->cis', matrices.astype(jnp.float32), gathered)
        assembled = jnp.zeros((NODE_DEV + FACE, band_width), jnp.float32)
        return assembled.at[links.reshape(-1)].add(products.reshape(-1, band_width))
    assembled = lax.map(one_domain, (extended, cell_blocks, link_blocks))
    own_rows = assembled[:, :NODE_DEV]
    returned = jnp.concatenate([jnp.zeros_like(assembled[:1, NODE_DEV:]), assembled[:-1, NODE_DEV:]], axis=0)
    summed = jax.vmap(lambda target, picks, extra: target.at[picks].add(extra))(own_rows, face_lists, returned)
    return mass_scale[:, None] * summed.reshape(N_DOM * NODE_DEV, band_width)

def reference(wavefunctions, mass_scale, cell_matrices, connectivity, face_index):

    def hamiltonian(vectors):
        return apply_hamiltonian(vectors, mass_scale, cell_matrices, connectivity, face_index)
    previous = wavefunctions.astype(jnp.float32)
    current = (hamiltonian(previous) - 5.0 * previous) / 5.0
    for sweep_index in range(DEGREE - 1):
        following = 2.0 * (hamiltonian(current) - 5.0 * current) / 5.0 - previous
        previous, current = (current, following)
    filtered = current
    rounded = filtered.astype(jnp.bfloat16)
    margin = jnp.dot(rounded.T, rounded, preferred_element_type=jnp.float32) / (NODE_DEV * N_DOM)
    mean_eigen = jnp.trace(margin) / STATES
    identity = jnp.eye(STATES, dtype=jnp.float32)
    current_y = margin / mean_eigen
    current_z = identity
    highest = lax.Precision.HIGHEST
    for ns_index in range(NS_ITERS):
        product = jnp.dot(current_z, current_y, precision=highest, preferred_element_type=jnp.float32)
        correction = 1.5 * identity - 0.5 * product
        current_y = jnp.dot(current_y, correction, precision=highest, preferred_element_type=jnp.float32)
        current_z = jnp.dot(current_z, correction, precision=highest, preferred_element_type=jnp.float32)
    inverse_root = current_z / jnp.sqrt(mean_eigen)
    return jnp.dot(filtered, inverse_root, precision=highest, preferred_element_type=jnp.float32)
```

```python
import functools

import jax
import jax.numpy as jnp
from jax import lax
from jax.experimental import pallas as pl
from jax.experimental.pallas import tpu as pltpu
from jax.sharding import PartitionSpec as P

filter_center = 5.0
filter_half = 5.0
MESH = pl.DeviceIdType.MESH
VMEM_LIMIT = 62 * 1024 * 1024


def row_tile(rows, most):
    return max(t for t in range(16, most + 1, 16) if rows % t == 0)


def dot32(a, b, dims=((1,), (0,))):
    return lax.dot_general(a, b, (dims, ((), ())), preferred_element_type=jnp.float32)


def operator_kernel(share, conn_ref, a_ref, m_ref, ht, b, send_sem, recv_sem):
    cells, nodes = conn_ref.shape
    extent, width = m_ref.shape[1], b.shape[1]
    me = lax.axis_index("band") if share > 1 else 0
    if share > 1:
        barrier = pltpu.get_barrier_semaphore()
        for step in range(1, share):
            peer = lax.rem(me + step, share)
            pl.semaphore_signal(barrier, inc=1, device_id={"band": peer}, device_id_type=MESH)
        pl.semaphore_wait(barrier, share - 1)
    build = row_tile(extent, 256)

    @pl.loop(0, cells)
    def _(c):
        links = conn_ref[pl.ds(c, 1), :]
        span = pl.ds(pl.multiple_of(c * nodes, 128), nodes)

        @pl.loop(0, extent // build)
        def _(r):
            ids = lax.broadcasted_iota(jnp.int32, (build, nodes), 0) + r * build
            ht[pl.ds(pl.multiple_of(r * build, build), build), span] = jnp.where(
                ids == links, 1.0, 0.0
            ).astype(jnp.bfloat16)

    first = pl.multiple_of(me * width, 128) if share > 1 else 0

    @pl.loop(0, cells)
    def _(c):
        span = pl.ds(pl.multiple_of(c * nodes, 128), nodes)
        picks = ht[pl.ds(first, width), span]
        b[span, :] = dot32(a_ref[c], picks, ((1,), (1,))).astype(jnp.bfloat16)

    tile = row_tile(extent, 384)
    tiles = extent // tile

    def copies(r):
        rows = pl.ds(pl.multiple_of(r * tile, tile), tile)
        return [
            pltpu.make_async_remote_copy(
                src_ref=m_ref.at[me, rows],
                dst_ref=m_ref.at[me, rows],
                send_sem=send_sem.at[step, r],
                recv_sem=recv_sem.at[step, r],
                device_id={"band": lax.rem(me + step, share)},
                device_id_type=MESH,
            )
            for step in range(1, share)
        ]

    @pl.loop(0, tiles)
    def _(r):
        rows = pl.ds(pl.multiple_of(r * tile, tile), tile)
        total = dot32(ht[rows, :], b[...])
        kept = total.astype(jnp.bfloat16)
        m_ref[me, rows, :width] = kept
        offsets = lax.broadcasted_iota(jnp.int32, (tile, width), 1) - lax.broadcasted_iota(
            jnp.int32, (tile, width), 0
        )
        rest = jnp.where(
            offsets == r * tile - me * width, total - kept.astype(jnp.float32), 0.0
        )
        rest = jnp.sum(rest, axis=1, keepdims=True)
        m_ref[me, rows, width:] = jnp.broadcast_to(rest, (tile, 128)).astype(jnp.bfloat16)
        for copy in copies(r):
            copy.start()

    @pl.loop(0, tiles)
    def _(r):
        for copy in copies(r):
            copy.wait()


def domain_operator(cell_matrices, connectivity, extent):
    cells, nodes = connectivity.shape
    share = lax.axis_size("band")
    if extent % (share * 128):
        share = 1
    width = extent // share
    tiles = extent // row_tile(extent, 384)
    vmem = pl.BlockSpec(memory_space=pltpu.VMEM)
    params = dict(collective_id=0, has_side_effects=True) if share > 1 else {}
    halves = pl.pallas_call(
        functools.partial(operator_kernel, share),
        out_shape=jax.ShapeDtypeStruct((share, extent, width + 128), jnp.bfloat16),
        in_specs=[vmem] * 2,
        out_specs=vmem,
        scratch_shapes=[
            pltpu.VMEM((extent, cells * nodes), jnp.bfloat16),
            pltpu.VMEM((cells * nodes, width), jnp.bfloat16),
            pltpu.SemaphoreType.DMA((share, tiles)),
            pltpu.SemaphoreType.DMA((share, tiles)),
        ],
        compiler_params=pltpu.CompilerParams(vmem_limit_bytes=VMEM_LIMIT, **params),
        name="domain_operator",
    )(connectivity, cell_matrices)
    rest = sum(halves[i, :, width:].astype(jnp.float32) for i in range(share))
    return jnp.concatenate([halves[i, :, :width] for i in range(share)], axis=1), rest


def passed_along(value, axis, steps):
    count = lax.axis_size(axis)
    initial, last = (max(0, -steps), min(count, count - steps))
    return lax.ppermute(value, axis, [(source, source + steps) for source in range(initial, last)])


def on_device(wavefunctions, mass_scale, cell_matrices, connectivity, face_index):
    bf16 = jnp.bfloat16
    own, band_width = wavefunctions.shape
    face = face_index.shape[0]
    domains = lax.axis_size("dom")
    states = band_width * lax.axis_size("band")
    matrix, rest = domain_operator(cell_matrices, connectivity, own + face)
    face_of = (face_index[:, None] == lax.broadcasted_iota(jnp.int32, (face, own), 1)).astype(bf16)
    face_in = (face_index[None, :] == lax.broadcasted_iota(jnp.int32, (own, face), 0)).astype(bf16)
    outgoing = jnp.concatenate([matrix[own:, :own], face_of], axis=0)
    inner = matrix[:own, :own]
    edge = jnp.concatenate([matrix[:own, own:], face_in, face_in], axis=1)
    corner = jnp.concatenate([matrix[own:, own:], rest[own:].astype(bf16)], axis=1)
    corner = passed_along(corner, "dom", 1)
    corner, corner_rest = corner[:, :face], corner[:, face : face + 1].astype(jnp.float32)
    rest = rest[:own, :1]
    mass = mass_scale[:, None]

    def hamiltonian(vectors):
        scaled = (mass * vectors).astype(bf16)
        sent = dot32(outgoing, scaled).astype(bf16)
        returned = passed_along(sent[:face], "dom", 1)
        received = passed_along(sent[face:], "dom", -1)
        summed = dot32(inner, scaled) + rest * scaled.astype(jnp.float32)
        added = returned.astype(jnp.float32) + dot32(corner, sent[face:])
        added = added + corner_rest * sent[face:].astype(jnp.float32)
        high = added.astype(bf16)
        low = (added - lax.reduce_precision(added, 8, 7)).astype(bf16)
        summed = summed + dot32(edge, jnp.concatenate([received, high, low], axis=0))
        return mass * summed

    previous = wavefunctions.astype(jnp.float32)
    current = (hamiltonian(previous) - filter_center * previous) / filter_half
    for _ in range(2):
        following = 2.0 * (hamiltonian(current) - filter_center * current) / filter_half - previous
        previous, current = (current, following)
    rounded = current.astype(bf16)
    everyone = lax.all_gather(rounded, "band", axis=1, tiled=True)
    partial = dot32(everyone, rounded, ((0,), (0,))) / (own * domains)
    tile = lax.psum_scatter(partial.astype(bf16), "dom", scatter_dimension=0, tiled=True)
    columns = lax.all_gather(tile, "dom", axis=0, tiled=True)
    margin = lax.all_gather(columns, "band", axis=1, tiled=True).astype(jnp.float32)
    identity = (
        lax.broadcasted_iota(jnp.int32, (states, states), 0)
        == lax.broadcasted_iota(jnp.int32, (states, states), 1)
    ).astype(jnp.float32)
    mean_eigen = jnp.sum(margin * identity) / states
    offset = (margin / mean_eigen - identity).astype(bf16)
    start = lax.axis_index("band") * band_width
    first = lax.dynamic_slice_in_dim(columns.astype(jnp.float32), 0, states, 0) / mean_eigen
    first = first - lax.dynamic_slice_in_dim(identity, start, band_width, 1)
    second = dot32(offset, first.astype(bf16))
    third = dot32(offset, second.astype(bf16))
    tail = dot32(offset, (third / 16.0 - second * (5.0 / 16.0)).astype(bf16))
    change = tail + 0.375 * second - 0.5 * first
    turned = current + dot32(everyone, change.astype(bf16))
    return turned / jnp.sqrt(mean_eigen)


def solution(mesh):
    return jax.shard_map(
        on_device,
        mesh=mesh,
        in_specs=(P("dom", "band"), P("dom"), P("dom", None, None), P("dom", None), P("dom")),
        out_specs=P("dom", "band"),
        check_vma=False,
    )
```
